32 devices in a mesh: outer: 16 (over z, x, core), inner: 2 (over y).
Axes of the slice: x: 2, y: 2, z: 4, core: 2. Of those that a mesh axis runs over, the one named last changes fastest.
Arguments:
- picture_feature_array: float32 [4096, 1152], P(('outer', 'inner')), may hold values from -0.4 to 0.4
- caption_hidden_activations: float32 [4096, 1152], P(('outer', 'inner')), may hold values from -0.8 to 0.8
- normalizer_multiplier: float32 [1152], replicated, may hold values from 0.5 to 1.5
- normalizer_shift: float32 [1152], replicated, may hold values from -3 to 3
- caption_head_matrix: bfloat16 [1152, 1152], P(None, 'inner'), may hold values from -0.1875 to 0.1875
- similarity_sharpness: float32 [1], replicated, may hold values from 4 to 16
- similarity_shift: float32 [1], replicated, may hold values from -3 to -1
Outputs:
- row_loss: float32 [4096], P(('outer', 'inner'))
- image_grad: float32 [4096, 1152], P(('outer', 'inner'))
- text_grad: float32 [4096, 1152], P(('outer', 'inner'))
The draws below stay inside these ranges and needn't reach their ends.
All inputs are finite; a program needn't handle non-finite values.
Results may differ from the reference program's by a relative error of at most 0.0085.
Values may be sent and summed in bfloat16 or wider, within the bound.
No kernel may reach another device: no remote copies, remote signals or barrier semaphores. Data moves between devices by JAX's collectives and lax.ppermute only.
A program may use at most 64 MiB of HBM per device.

```python
import math
import jax
import jax.numpy as jnp
from jax import lax

EMBED_WIDTH = 1152
ROWS_DEV = 128
BLOCKS = 3
TOTAL_ROWS = 4096
N_OUTER = 16
N_INNER = 2


def block_scale(own_key, dims, shards, low, high):
    gain, own = 1.0, jax.random.fold_in(own_key, 6)
    for axis_at, shards_of in shards:
        steps = jnp.exp(jax.random.uniform(jax.random.fold_in(own, axis_at), (shards_of,), jnp.float32, low / len(shards), high / len(shards)))
        gain = gain * jnp.repeat(steps, dims[axis_at] // shards_of).reshape([-1 if axis == axis_at else 1 for axis in range(len(dims))])
    return gain


def noise(stream_key, shape, scale, bound, cuts=(), kind=jnp.bfloat16):
    values = jax.random.normal(stream_key, shape, jnp.float32) * scale
    if len(cuts) > 0:
        values = block_scale(stream_key, shape, cuts, -0.22, 0.18) * values
    return jnp.clip(values, min=-bound, max=bound).astype(kind)


def setup_inputs(seed: int = 0) -> dict:
    keys = jax.random.split(jax.random.key(seed), 8)
    picture_feature_array = noise(keys[0], (TOTAL_ROWS, EMBED_WIDTH), 0.05, 0.4, ((0, 32),), jnp.float32)
    caption_hidden_activations = noise(keys[1], (TOTAL_ROWS, EMBED_WIDTH), 0.1, 0.8, ((0, 32),), jnp.float32)
    normalizer_multiplier = jnp.clip(1.0 + 0.1 * jax.random.normal(keys[2], (EMBED_WIDTH,), jnp.float32), 0.5, 1.5)
    normalizer_shift = noise(keys[3], (EMBED_WIDTH,), 0.5, 3.0, (), jnp.float32)
    caption_head_matrix = noise(keys[4], (EMBED_WIDTH, EMBED_WIDTH), EMBED_WIDTH ** -0.5, 0.1875, ((1, 2),))
    similarity_sharpness = jnp.clip(jnp.exp(jax.random.uniform(keys[5], (1,), jnp.float32, math.log(4.0), math.log(16.0))), 4.0, 16.0)
    similarity_shift = jnp.clip(jax.random.uniform(keys[6], (1,), jnp.float32, -3.0, -1.0), -3.0, -1.0)
    return dict(picture_feature_array=picture_feature_array, caption_hidden_activations=caption_hidden_activations, normalizer_multiplier=normalizer_multiplier, normalizer_shift=normalizer_shift, caption_head_matrix=caption_head_matrix, similarity_sharpness=similarity_sharpness, similarity_shift=similarity_shift)


EPSILON = 1e-06

def unit_rows(values):
    lengths = jnp.sqrt(lax.optimization_barrier(jnp.sum(values * values, axis=-1, keepdims=True)) + EPSILON)
    return (values / lengths, lengths)

def layer_stats(hidden):
    average = lax.optimization_barrier(jnp.mean(hidden, axis=-1, keepdims=True))
    centred = hidden - average
    inverse = lax.rsqrt(lax.optimization_barrier(jnp.mean(centred * centred, axis=-1, keepdims=True)) + EPSILON)
    return (centred * inverse, inverse)

def pairwise_terms(image_unit_vectors, text_unit_vectors, multiplier_coefficient, block_offset, positive_mask):
    pair_logits = multiplier_coefficient * jnp.dot(image_unit_vectors, text_unit_vectors.T, preferred_element_type=jnp.float32) + block_offset
    labels = jnp.where(positive_mask, 1.0, -1.0).astype(jnp.float32)
    loss_values = jax.nn.softplus(-labels * pair_logits)
    logit_slopes = (-labels * jax.nn.sigmoid(-labels * pair_logits)).astype(jnp.bfloat16)
    return (loss_values, logit_slopes)

def reference(picture_feature_array, caption_hidden_activations, normalizer_multiplier, normalizer_shift, caption_head_matrix, similarity_sharpness, similarity_shift):
    multiplier_coefficient = similarity_sharpness[0]
    block_offset = similarity_shift[0]
    group_rows = ROWS_DEV * N_INNER
    image_dir, image_lengths = unit_rows(picture_feature_array)
    image_unit_vectors = image_dir.astype(jnp.bfloat16)
    standard, inverse = layer_stats(caption_hidden_activations)
    normed = (standard * normalizer_multiplier + normalizer_shift).astype(jnp.bfloat16)
    projected = jnp.dot(normed, caption_head_matrix, preferred_element_type=jnp.float32)
    text_dir, text_lengths = unit_rows(projected)
    text_unit_vectors = text_dir.astype(jnp.bfloat16)
    image_row_groups = image_unit_vectors.reshape(N_OUTER, group_rows, EMBED_WIDTH)
    text_row_groups = text_unit_vectors.reshape(N_OUTER, group_rows, EMBED_WIDTH)
    places = jnp.arange(group_rows, dtype=jnp.int32)
    positive_mask = places[:, None] == places[None, :]
    empty_pair_count = jnp.zeros_like(positive_mask)

    def image_side(group_number_index):
        loss_total = jnp.zeros((group_rows,), jnp.float32)
        total_gradient = jnp.zeros((group_rows, EMBED_WIDTH), jnp.float32)
        for visit_step in range(BLOCKS):
            text_batch = text_row_groups[(group_number_index - visit_step) % N_OUTER]
            loss_values, logit_slopes = pairwise_terms(image_row_groups[group_number_index], text_batch, multiplier_coefficient, block_offset, positive_mask if visit_step == 0 else empty_pair_count)
            loss_total = loss_total + lax.optimization_barrier(jnp.sum(loss_values, axis=1))
            total_gradient = total_gradient + jnp.dot(logit_slopes, text_batch, preferred_element_type=jnp.float32)
        return (loss_total, total_gradient)

    def text_side(group_number_index):
        total_gradient = jnp.zeros((group_rows, EMBED_WIDTH), jnp.float32)
        for visit_step in range(BLOCKS):
            image_batch = image_row_groups[(group_number_index + visit_step) % N_OUTER]
            loss_values, logit_slopes = pairwise_terms(image_batch, text_row_groups[group_number_index], multiplier_coefficient, block_offset, positive_mask if visit_step == 0 else empty_pair_count)
            total_gradient = total_gradient + jnp.dot(logit_slopes.T, image_batch, preferred_element_type=jnp.float32)
        return total_gradient
    indices = jnp.arange(N_OUTER, dtype=jnp.int32)
    loss_groups, image_gradient_sums = lax.map(image_side, indices)
    text_gradient_sums = lax.map(text_side, indices)
    row_loss = loss_groups.reshape(TOTAL_ROWS) / (BLOCKS * group_rows)
    image_normed_gradient = multiplier_coefficient * image_gradient_sums.reshape(TOTAL_ROWS, EMBED_WIDTH)
    text_normed_gradient = multiplier_coefficient * text_gradient_sums.reshape(TOTAL_ROWS, EMBED_WIDTH)
    image_grad = (image_normed_gradient - image_dir * lax.optimization_barrier(jnp.sum(image_dir * image_normed_gradient, axis=-1, keepdims=True))) / image_lengths
    proj_grad = ((text_normed_gradient - text_dir * lax.optimization_barrier(jnp.sum(text_dir * text_normed_gradient, axis=-1, keepdims=True))) / text_lengths).astype(jnp.bfloat16)
    normed_grad = lax.dot_general(proj_grad, caption_head_matrix, (((1,), (1,)), ((), ())), preferred_element_type=jnp.float32)
    scaled = normed_grad * normalizer_multiplier
    text_grad = inverse * (scaled - lax.optimization_barrier(jnp.mean(scaled, axis=-1, keepdims=True)) - standard * lax.optimization_barrier(jnp.mean(scaled * standard, axis=-1, keepdims=True)))
    return (row_loss, image_grad, text_grad)
```

```python
import jax
import jax.numpy as jnp
from jax import lax
from jax.experimental import pallas as pl
from jax.experimental.pallas import tpu as pltpu
from jax.sharding import PartitionSpec as P

BLOCKS = 3


EPSILON = 1e-06


def from_behind(value, axis, steps):
    count = lax.axis_size(axis)
    pairs = [(source, (source + steps) % count) for source in range(count)]
    return lax.ppermute(value, axis, pairs)


def unit_rows(values):
    lengths = jnp.sqrt(jnp.sum(values * values, axis=-1, keepdims=True) + EPSILON)
    return (values / lengths, lengths)


def layer_stats(hidden):
    average = jnp.mean(hidden, axis=-1, keepdims=True)
    centred = hidden - average
    inverse = lax.rsqrt(jnp.mean(centred * centred, axis=-1, keepdims=True) + EPSILON)
    return (centred * inverse, inverse)


def pairwise_terms(
    image_unit_vectors, text_unit_vectors, multiplier_coefficient, block_offset, positive_mask
):
    pair_logits = (
        multiplier_coefficient
        * lax.dot_general(
            image_unit_vectors,
            text_unit_vectors,
            (((1,), (1,)), ((), ())),
            preferred_element_type=jnp.float32,
        )
        + block_offset
    )
    labels = jnp.where(positive_mask, 1.0, -1.0).astype(jnp.float32)
    loss_values = jax.nn.softplus(-labels * pair_logits)
    logit_slopes = (-labels * jax.nn.sigmoid(-labels * pair_logits)).astype(jnp.bfloat16)
    return (loss_values, logit_slopes)


def on_device(
    picture_feature_array,
    caption_hidden_activations,
    normalizer_multiplier,
    normalizer_shift,
    caption_head_matrix,
    similarity_sharpness,
    similarity_shift,
):
    multiplier_coefficient = similarity_sharpness[0]
    block_offset = similarity_shift[0]
    rows_here = picture_feature_array.shape[0]
    features = picture_feature_array.shape[1]
    image_dir, image_lengths = unit_rows(picture_feature_array)
    image_unit_vectors = image_dir.astype(jnp.bfloat16)
    standard, inverse = layer_stats(caption_hidden_activations)
    normed = (standard * normalizer_multiplier + normalizer_shift).astype(jnp.bfloat16)
    full_proj = lax.all_gather(caption_head_matrix, "inner", axis=1, tiled=True)
    projected = jnp.dot(normed, full_proj, preferred_element_type=jnp.float32)
    text_dir, text_lengths = unit_rows(projected)
    text_unit_vectors = text_dir.astype(jnp.bfloat16)
    image_group = lax.all_gather(image_unit_vectors, "inner", axis=0, tiled=True)
    group_rows = image_group.shape[0]
    row_ids = lax.broadcasted_iota(jnp.int32, (rows_here, group_rows), 0)
    columns = lax.broadcasted_iota(jnp.int32, (rows_here, group_rows), 1)
    positive_mask = columns == row_ids + lax.axis_index("inner") * rows_here
    empty_pair_count = jnp.zeros_like(positive_mask)
    text_block = lax.all_gather(text_unit_vectors, "inner", axis=0, tiled=True)
    block_list = [text_block]
    for visit_step in range(1, BLOCKS):
        text_block = from_behind(text_block, "outer", 1)
        block_list.append(text_block)
    loss_total = jnp.zeros((rows_here,), jnp.float32)
    total_gradient = jnp.zeros((rows_here, features), jnp.float32)
    slope_list = []
    for visit_step in range(BLOCKS):
        loss_values, logit_slopes = pairwise_terms(
            image_unit_vectors,
            block_list[visit_step],
            multiplier_coefficient,
            block_offset,
            positive_mask if visit_step == 0 else empty_pair_count,
        )
        loss_total = loss_total + jnp.sum(loss_values, axis=1)
        total_gradient = total_gradient + jnp.dot(
            logit_slopes, block_list[visit_step], preferred_element_type=jnp.float32
        )
        slope_list.append(logit_slopes)
    own_pairs = jnp.transpose(positive_mask)
    none_here = jnp.zeros_like(own_pairs)
    moving_images = image_unit_vectors
    visitors = image_group
    text_gradient_sums = jnp.zeros((rows_here, features), jnp.float32)
    for visit_step in range(BLOCKS):
        if visit_step > 0:
            moving_images = from_behind(moving_images, "outer", -1)
            visitors = lax.all_gather(moving_images, "inner", axis=0, tiled=True)
        unused, back_slopes = pairwise_terms(
            visitors,
            text_unit_vectors,
            multiplier_coefficient,
            block_offset,
            own_pairs if visit_step == 0 else none_here,
        )
        text_gradient_sums = text_gradient_sums + lax.dot_general(
            back_slopes, visitors, (((0,), (0,)), ((), ())), preferred_element_type=jnp.float32
        )
    row_loss = loss_total / (BLOCKS * group_rows)
    image_normed_gradient = multiplier_coefficient * total_gradient
    text_normed_gradient = multiplier_coefficient * text_gradient_sums
    image_grad = (
        image_normed_gradient
        - image_dir * jnp.sum(image_dir * image_normed_gradient, axis=-1, keepdims=True)
    ) / image_lengths
    proj_grad = (
        (
            text_normed_gradient
            - text_dir * jnp.sum(text_dir * text_normed_gradient, axis=-1, keepdims=True)
        )
        / text_lengths
    ).astype(jnp.bfloat16)
    normed_grad = lax.dot_general(
        proj_grad, full_proj, (((1,), (1,)), ((), ())), preferred_element_type=jnp.float32
    )
    scaled = normed_grad * normalizer_multiplier
    text_grad = inverse * (
        scaled
        - jnp.mean(scaled, axis=-1, keepdims=True)
        - standard * jnp.mean(scaled * standard, axis=-1, keepdims=True)
    )
    return (row_loss, image_grad, text_grad)


NT = (((1,), (1,)), ((), ()))
NN = (((1,), (0,)), ((), ()))


def whole(kernel, out_shape, *operands, scratch=(), scalars=0, name=None):
    vmem = pl.BlockSpec(memory_space=pltpu.VMEM)
    smem = pl.BlockSpec(memory_space=pltpu.SMEM)
    specs = [smem] * scalars + [vmem] * (len(operands) - scalars)
    return pl.pallas_call(
        kernel,
        in_specs=specs,
        out_specs=jax.tree.map(lambda _: vmem, out_shape),
        out_shape=out_shape,
        scratch_shapes=list(scratch),
        name=name,
    )(*operands)


def inverse_length(values):
    return lax.rsqrt(jnp.sum(values * values, axis=-1, keepdims=True) + EPSILON)


def standardised(hidden):
    average = jnp.mean(hidden, axis=-1, keepdims=True)
    centred = hidden - average
    inverse = lax.rsqrt(jnp.mean(centred * centred, axis=-1, keepdims=True) + EPSILON)
    return (centred * inverse, inverse)


def loss_and_slopes(logits, positive):
    signed = logits if positive is None else jnp.where(positive, -logits, logits)
    small = jnp.exp(-jnp.abs(signed))
    loss = jnp.maximum(signed, 0.0) + jnp.log1p(small)
    slope = jnp.where(signed >= 0.0, 1.0, small) / (1.0 + small)
    if positive is not None:
        slope = jnp.where(positive, -slope, slope)
    return (loss, slope.astype(jnp.bfloat16))


def diagonal(rows, columns):
    return lax.broadcasted_iota(jnp.int32, (rows, columns), 0) == lax.broadcasted_iota(
        jnp.int32, (rows, columns), 1
    )


def prepare(picture, hidden, gain, shift, image_units, normed):
    values = picture[...]
    image_units[...] = (values * inverse_length(values)).astype(jnp.bfloat16)
    standard, _ = standardised(hidden[...])
    normed[...] = (standard * gain[...] + shift[...]).astype(jnp.bfloat16)


def image_side(place, sharp, offset, *refs):
    pieces = refs[:4]
    texts = refs[4:7]
    images = refs[7:9]
    head, units, projected, own_grad, sent_grad, losses = refs[9:15]
    normed, all_units = refs[15:]
    half = pieces[0].shape[0]
    rows = texts[0].shape[0]
    step = pieces[1].shape[0]
    at = 0
    for piece in pieces:
        size = half if piece.shape[0] == half else step
        for start in range(0, piece.shape[0], size):
            head[pl.ds(pl.multiple_of(place[at], 16), size), :] = piece[start : start + size, :]
            at += 1
    for block, text in enumerate(texts):
        normed[block * rows : (block + 1) * rows, :] = text[...]
    result = lax.dot_general(normed[...], head[...], NT, preferred_element_type=jnp.float32)
    projected[...] = result[:rows]
    all_units[...] = (result * inverse_length(result)).astype(jnp.bfloat16)
    units[...] = all_units[:rows, :]
    loss_sums = []
    for side, image in enumerate(images):
        logits = (
            sharp[0]
            * lax.dot_general(image[...], all_units[...], NT, preferred_element_type=jnp.float32)
            + offset[0]
        )
        positive = diagonal(*logits.shape) if side == 0 else None
        loss, slopes = loss_and_slopes(logits, positive)
        grad = lax.dot_general(slopes, all_units[...], NN, preferred_element_type=jnp.float32)
        if side == 0:
            own_grad[...] = grad
        else:
            sent_grad[...] = grad.astype(jnp.bfloat16)
        loss_sums.append(jnp.sum(loss, axis=1, keepdims=True))
    for side, total in enumerate(loss_sums):
        spread = jnp.transpose(jnp.broadcast_to(total, (rows, 128)))
        losses[side * 8 : side * 8 + 8, :] = spread[0:8, :]


def text_side(core, sharp, offset, units, projected, head, hidden, gain, *refs):
    images, text_grad, block = refs[:8], refs[8], refs[9]
    rows = units.shape[0]
    own, other, mid_a0, mid_b0, mid_a1, mid_b1, far_a, far_b = images
    upper = core[0] == 1
    block[0 * rows : 1 * rows, :] = own[...]
    block[1 * rows : 2 * rows, :] = other[...]
    block[2 * rows : 3 * rows, :] = jnp.where(upper, mid_a1[...], mid_a0[...])
    block[3 * rows : 4 * rows, :] = jnp.where(upper, mid_b1[...], mid_b0[...])
    block[4 * rows : 5 * rows, :] = far_a[...]
    block[5 * rows : 6 * rows, :] = far_b[...]
    logits = (
        sharp[0]
        * lax.dot_general(units[...], block[...], NT, preferred_element_type=jnp.float32)
        + offset[0]
    )
    _, slopes = loss_and_slopes(logits, diagonal(*logits.shape))
    grad = sharp[0] * lax.dot_general(slopes, block[...], NN, preferred_element_type=jnp.float32)
    values = projected[...]
    over = inverse_length(values)
    text_dir = values * over
    inward = (grad - text_dir * jnp.sum(text_dir * grad, axis=-1, keepdims=True)) * over
    scaled = (
        lax.dot_general(
            inward.astype(jnp.bfloat16), head[...], NN, preferred_element_type=jnp.float32
        )
        * gain[...]
    )
    standard, inverse = standardised(hidden[...])
    text_grad[...] = inverse * (
        scaled
        - jnp.mean(scaled, axis=-1, keepdims=True)
        - standard * jnp.mean(scaled * standard, axis=-1, keepdims=True)
    )


def finish(sharp, picture, own_grad, got_grad, own_loss, got_loss, image_grad, row_loss):
    values = picture[...]
    over = inverse_length(values)
    image_dir = values * over
    grad = sharp[0] * (own_grad[...] + got_grad[...].astype(jnp.float32))
    image_grad[...] = (grad - image_dir * jnp.sum(image_dir * grad, axis=-1, keepdims=True)) * over
    pairs = BLOCKS * 2 * values.shape[0]
    row_loss[...] = (own_loss[0:1, :] + got_loss[0:1, :]) / pairs


def on_pair(
    picture_feature_array,
    caption_hidden_activations,
    normalizer_multiplier,
    normalizer_shift,
    caption_head_matrix,
    similarity_sharpness,
    similarity_shift,
):
    count = lax.axis_size("outer")
    group = lax.axis_index("outer")
    inner = lax.axis_index("inner")
    core = group % 2
    rows, features = picture_feature_array.shape

    def move(value, to, label):
        pairs = []
        for outer_at in range(count):
            for inner_at in range(2):
                outer_to, inner_to = to(outer_at, inner_at)
                pairs.append((outer_at * 2 + inner_at, (outer_to % count) * 2 + inner_to))
        with jax.named_scope(label):
            return lax.ppermute(value, ("outer", "inner"), pairs)

    across = lambda o, i: (o, 1 - i)
    partner = lambda o, i: (o ^ 1, i)
    gain = normalizer_multiplier.reshape(1, features)
    shift = normalizer_shift.reshape(1, features)
    like = lambda shape, dtype: jax.ShapeDtypeStruct(shape, dtype)

    head_own = caption_head_matrix.T
    half = head_own.shape[0]
    quarter = half // 4
    flip = (group // 4) % 2
    mine = lax.dynamic_slice(head_own, ((core * 2 + flip) * quarter, 0), (quarter, features))
    head_y = move(mine, across, "head_y")
    head_z = move(head_y, lambda o, i: (o ^ 4, i), "head_z")
    two = jnp.concatenate([head_y, head_z], axis=0)
    head_c = move(two, partner, "head_c")

    image_own, text_own = whole(
        prepare,
        (like((rows, features), jnp.bfloat16), like((rows, features), jnp.bfloat16)),
        picture_feature_array,
        caption_hidden_activations,
        gain,
        shift,
        name="prepare",
    )
    text_far = move(text_own, lambda o, i: (o + 2, i), "text_far")
    image_across = move(image_own, across, "image_across")
    image_far = move(image_own, lambda o, i: (o - 2, i), "image_far")
    image_far_across = move(image_across, lambda o, i: (o - 2, i), "image_far_across")
    chip_text_own = move(text_own, partner, "chip_text_own")
    chip_text_far = move(text_far, partner, "chip_text_far")
    chip_image_own = move(image_own, partner, "chip_image_own")
    chip_image_across = move(image_across, partner, "chip_image_across")
    chip_image_far = move(image_far, partner, "chip_image_far")
    chip_image_far_across = move(image_far_across, partner, "chip_image_far_across")
    text_mid = jnp.where(core == 1, chip_text_own, chip_text_far)

    other = (1 - inner) * half
    place = jnp.stack(
        [
            inner * half,
            other + (core * 2 + flip) * quarter,
            other + (core * 2 + 1 - flip) * quarter,
            other + ((1 - core) * 2 + flip) * quarter,
            other + ((1 - core) * 2 + 1 - flip) * quarter,
        ]
    ).astype(jnp.int32)

    head, units, projected, own_grad, sent_grad, losses = whole(
        image_side,
        (
            like((features, features), jnp.bfloat16),
            like((rows, features), jnp.bfloat16),
            like((rows, features), jnp.float32),
            like((rows, features), jnp.float32),
            like((rows, features), jnp.bfloat16),
            like((16, rows), jnp.float32),
        ),
        place,
        similarity_sharpness,
        similarity_shift,
        head_own,
        head_y,
        head_z,
        head_c,
        text_own,
        text_mid,
        text_far,
        image_own,
        image_across,
        scratch=(
            pltpu.VMEM((3 * rows, features), jnp.bfloat16),
            pltpu.VMEM((3 * rows, features), jnp.bfloat16),
        ),
        scalars=3,
        name="image_side",
    )
    got_grad = move(sent_grad, across, "late_grad")
    got_loss = move(losses[8:], across, "late_loss")
    text_grad = whole(
        text_side,
        like((rows, features), jnp.float32),
        core.reshape(1).astype(jnp.int32),
        similarity_sharpness,
        similarity_shift,
        units,
        projected,
        head,
        caption_hidden_activations,
        gain,
        image_own,
        image_across,
        chip_image_own,
        chip_image_across,
        chip_image_far,
        chip_image_far_across,
        image_far,
        image_far_across,
        scratch=(pltpu.VMEM((6 * rows, features), jnp.bfloat16),),
        scalars=3,
        name="text_side",
    )
    image_grad, row_loss = whole(
        finish,
        (like((rows, features), jnp.float32), like((1, rows), jnp.float32)),
        similarity_sharpness,
        picture_feature_array,
        own_grad,
        got_grad,
        losses[:8],
        got_loss,
        scalars=1,
        name="finish",
    )
    return (row_loss.reshape(rows), image_grad, text_grad)


def solution(mesh):
    outer, inner = mesh.shape["outer"], mesh.shape["inner"]
    paired = inner == 2 and outer % 8 == 0

    in_specs = (
        P(("outer", "inner"), None),
        P(("outer", "inner"), None),
        P(),
        P(),
        P(None, "inner"),
        P(),
        P(),
    )
    out_specs = (P(("outer", "inner")), P(("outer", "inner"), None), P(("outer", "inner"), None))
    return jax.shard_map(
        on_pair if paired else on_device, mesh=mesh, in_specs=in_specs, out_specs=out_specs, check_vma=False
    )
```
